32 devices in a mesh: src: 8 (over z, y), tgt: 4 (over x, core).
Axes of the slice: x: 2, y: 2, z: 4, core: 2. Of those that a mesh axis runs over, the one named last changes fastest.
Arguments:
- edge_state: bfloat16 [65536, 512], P(('src', 'tgt')), may hold values from -6 to 6
- atom_state: bfloat16 [8192, 512], P('src'), may hold values from -6 to 6
- edge_src: int32 [65536], P(('src', 'tgt')), may hold values from 0 to 1023, as said below
- edge_tgt: int32 [65536], P(('src', 'tgt')), may hold values from 0 to 1023, as said below
- reverse: int32 [65536], P(('src', 'tgt')), may hold values from 0 to 2047, as said below
- w_in: bfloat16 [3, 512, 512], replicated, may hold values from -0.25 to 0.25
- w_out: bfloat16 [3, 512, 512], replicated, may hold values from -0.25 to 0.25
- edge_gain: float32 [3, 512], replicated, may hold values from 0.25 to 1.75
- atom_gain: float32 [512], replicated, may hold values from 0.25 to 1.75
- atom_up: bfloat16 [512, 512], replicated, may hold values from -0.25 to 0.25
- atom_down: bfloat16 [512, 512], replicated, may hold values from -0.25 to 0.25
Outputs:
- edge_out: bfloat16 [65536, 512], P(('src', 'tgt'))
The draws below stay inside these ranges and needn't reach their ends.
Inputs may be any that keep to these rules, and one draw needn't show every extreme that they name: edge_src is a local atom index within the edge's source block of 1024 atoms. edge_tgt is a local atom index within the edge's target block; the reverse edge's edge_src equals it. reverse is an involution on edges as defined in the reference program: the partner's partner is the edge itself, its source and target atoms are the edge's target and source, no edge is its own partner.
All inputs are finite; a program needn't handle non-finite values.
Results may differ from the reference program's by a relative error of at most 0.0075.
Values may be sent and summed in bfloat16 or wider, within the bound.
A program may use at most 64 MiB of HBM per device.

```python
import jax
import jax.numpy as jnp
from jax import lax

W = 512
BLOCKS = 3
E_DEV = 2048
AB = 1024
C = 2
Q = 128
ATOMS = 8192
EDGES = 65536
N_SRC = 8
N_TGT = 4


def graph_tables(key):
    count = N_SRC
    rows_sub = N_SRC * Q
    key_order = jax.random.fold_in(key, 11)
    key_ids = jax.random.fold_in(key, 12)
    scores = jax.random.randint(key_order, (count, count, rows_sub), 0, 65536) * rows_sub + jnp.arange(rows_sub, dtype=jnp.int32)
    order = jnp.argsort(scores, axis=-1).astype(jnp.int32)
    inverse = jnp.argsort(order, axis=-1).astype(jnp.int32)
    diagonal_pairs = jnp.take_along_axis(order, inverse ^ 1, axis=-1)
    first = jnp.arange(count, dtype=jnp.int32)[:, None, None]
    second = jnp.arange(count, dtype=jnp.int32)[None, :, None]
    pairing = jnp.where(first < second, order, jnp.where(first > second, jnp.transpose(inverse, (1, 0, 2)), diagonal_pairs))
    source_ids = jax.random.randint(key_ids, (count, count, rows_sub), 0, AB)
    target_ids = jnp.take_along_axis(jnp.transpose(source_ids, (1, 0, 2)), pairing, axis=-1)
    return (pairing, source_ids, target_ids)


def to_devices(table):
    shaped = table.reshape(N_SRC, N_TGT, C, N_SRC, Q)
    return jnp.transpose(shaped, (0, 1, 3, 2, 4)).reshape(-1).astype(jnp.int32)


def draw_edge_src(key, part):
    pairing, source_ids, target_ids = graph_tables(key)
    return to_devices(source_ids)


def draw_edge_tgt(key, part):
    pairing, source_ids, target_ids = graph_tables(key)
    return to_devices(target_ids)


def draw_reverse(key, part):
    pairing, source_ids, target_ids = graph_tables(key)
    subtile = (jnp.arange(N_SRC, dtype=jnp.int32) % C)[None, :, None]
    local = (pairing // Q * C + subtile) * Q + pairing % Q
    return to_devices(local)


def levels(rng, dims, pieces, low, high):
    loudness = 1.0
    for dim, blocks in pieces:
        steps = jax.random.uniform(jax.random.fold_in(jax.random.fold_in(rng, 6), dim), (blocks,), jnp.float32, low / len(pieces), high / len(pieces))
        loudness = loudness * jnp.repeat(jnp.exp(steps), dims[dim] // blocks).reshape((-1,) + (1,) * (len(dims) - 1 - dim))
    return loudness


def centred(own_key, extent, spread, limit, shards=(), kind=jnp.bfloat16):
    result = spread * jax.random.normal(own_key, extent, jnp.float32)
    if shards:
        result = result * levels(own_key, extent, shards, -0.22, 0.18)
    return jnp.clip(result, -limit, limit).astype(kind)


def setup_inputs(seed: int = 0) -> dict:
    key_of = jax.random.split(jax.random.key(seed), 12)
    return {
        "edge_state": centred(key_of[0], (EDGES, W), 1.0, 6.0, ((0, 32),)),
        "atom_state": centred(key_of[1], (ATOMS, W), 1.0, 6.0, ((0, 8),)),
        "edge_src": draw_edge_src(jax.random.fold_in(key_of[11], 71), 0),
        "edge_tgt": draw_edge_tgt(jax.random.fold_in(key_of[11], 71), 0),
        "reverse": draw_reverse(jax.random.fold_in(key_of[11], 71), 0),
        "w_in": centred(key_of[5], (BLOCKS, W, W), W ** -0.5, 0.25),
        "w_out": centred(key_of[6], (BLOCKS, W, W), W ** -0.5, 0.25),
        "edge_gain": jnp.clip(1.0 + 0.15 * jax.random.normal(key_of[7], (BLOCKS, W), jnp.float32), 0.25, 1.75),
        "atom_gain": jnp.clip(1.0 + 0.15 * jax.random.normal(key_of[8], (W,), jnp.float32), 0.25, 1.75),
        "atom_up": centred(key_of[9], (W, W), W ** -0.5, 0.25),
        "atom_down": centred(key_of[10], (W, W), W ** -0.5, 0.25),
    }


def rms_scaled(values, scales):
    return values * lax.rsqrt(lax.optimization_barrier(jnp.mean(values * values, axis=-1, keepdims=True)) + 1e-06) * scales

def reference(edge_state, atom_state, edge_src, edge_tgt, reverse, w_in, w_out, edge_gain, atom_gain, atom_up, atom_down):
    positions = jnp.arange(EDGES, dtype=jnp.int32)
    device_idx = positions // E_DEV
    local_pos = positions % E_DEV
    grid_row = device_idx // N_TGT
    grid_col = device_idx % N_TGT
    subtile = local_pos // Q % C
    source_atom = grid_row * AB + edge_src
    target_block = grid_col * C + subtile
    target_atom = (target_block * AB + edge_tgt).astype(jnp.int32)
    slice_idx = reverse // (C * Q)
    inner_row = reverse % Q
    partner = ((target_block * N_TGT + grid_row // C) * E_DEV + (slice_idx * C + grid_row % C) * Q + inner_row).astype(jnp.int32)
    initial = (edge_state.astype(jnp.float32) + atom_state[source_atom].astype(jnp.float32)).astype(jnp.bfloat16)
    mirrored = initial[partner]
    devices = N_SRC * N_TGT

    def edge_block(pair):
        start_rows, partner_rows = pair
        stream = start_rows.astype(jnp.float32)
        for layer in range(BLOCKS):
            normed = rms_scaled(stream, edge_gain[layer]).astype(jnp.bfloat16)
            hidden = jax.nn.silu(jnp.dot(normed, w_in[layer], preferred_element_type=jnp.float32)).astype(jnp.bfloat16)
            stream = stream + jnp.dot(hidden, w_out[layer], preferred_element_type=jnp.float32)
        return stream + partner_rows.astype(jnp.float32)
    merged = lax.map(edge_block, (initial.reshape(devices, E_DEV, W), mirrored.reshape(devices, E_DEV, W))).reshape(EDGES, W)
    message = merged.astype(jnp.bfloat16)
    atom_sum = jax.ops.segment_sum(message.astype(jnp.float32), target_atom, num_segments=ATOMS)
    atom_normed = rms_scaled(atom_sum, atom_gain).astype(jnp.bfloat16)
    atom_hidden = jax.nn.silu(jnp.dot(atom_normed, atom_up, preferred_element_type=jnp.float32)).astype(jnp.bfloat16)
    atom_new = jnp.dot(atom_hidden, atom_down, preferred_element_type=jnp.float32).astype(jnp.bfloat16)
    return (merged + atom_new[target_atom].astype(jnp.float32)).astype(jnp.bfloat16)
```

```python
import functools

import jax
import jax.numpy as jnp
from jax import lax
from jax.experimental import pallas as pl
from jax.experimental.pallas import tpu as pltpu
from jax.sharding import PartitionSpec as P

F32 = jnp.float32
BF16 = jnp.bfloat16


def rms_scaled(values, scales):
    return values * lax.rsqrt(jnp.mean(values * values, axis=-1, keepdims=True) + 1e-06) * scales


def picks(column, width):
    slots = lax.broadcasted_iota(jnp.int32, (column.shape[0], width), 1)
    return jnp.where(slots == column, 1.0, 0.0).astype(BF16)


def start_kernel(order, edge_ref, cols_ref, atom_ref, start_ref):
    rows, width = start_ref.shape
    sources = jnp.dot(picks(cols_ref[0, :, 0:1], atom_ref.shape[0]), atom_ref[...], preferred_element_type=F32)
    edges = edge_ref[...].reshape(rows, width).astype(F32)
    start_ref[...] = (edges + sources).astype(BF16)


def stream_kernel(start_ref, w_in_ref, w_out_ref, gain_ref, u_ref):
    stream = start_ref[...].astype(F32)
    for layer in range(w_in_ref.shape[0]):
        normed = rms_scaled(stream, gain_ref[layer : layer + 1]).astype(BF16)
        hidden = jax.nn.silu(jnp.dot(normed, w_in_ref[layer], preferred_element_type=F32)).astype(BF16)
        stream = stream + jnp.dot(hidden, w_out_ref[layer], preferred_element_type=F32)
    u_ref[...] = stream


def merge_kernel(groups, order, *refs):
    u_refs, recv_refs = refs[:groups], refs[groups : 2 * groups]
    cols_ref, tgt_ref, merged_ref, part_ref, total = refs[2 * groups :]
    turn, tile = pl.program_id(0), pl.program_id(1)

    @pl.when(tile == 0)
    def _():
        total[...] = jnp.zeros_like(total)

    for s in range(groups):

        @pl.when(turn == s)
        def _():
            partner = jnp.dot(
                picks(cols_ref[0, :, 1:2], recv_refs[s].shape[0]), recv_refs[s][...], preferred_element_type=F32
            )
            merged = u_refs[s][...] + partner
            merged_ref[0] = merged
            slots = lax.broadcasted_iota(jnp.int32, (total.shape[0], merged.shape[0]), 0)
            chosen = jnp.where(slots == tgt_ref[0], 1.0, 0.0).astype(BF16)
            total[...] += jnp.dot(chosen, merged.astype(BF16), preferred_element_type=F32)

    @pl.when(tile == pl.num_programs(1) - 1)
    def _():
        part_ref[0] = total[...].astype(part_ref.dtype)


def atom_kernel(sum_ref, gain_ref, up_ref, down_ref, new_ref):
    normed = rms_scaled(sum_ref[...].astype(F32), gain_ref[...]).astype(BF16)
    hidden = jax.nn.silu(jnp.dot(normed, up_ref[...], preferred_element_type=F32)).astype(BF16)
    new_ref[...] = jnp.dot(hidden, down_ref[...], preferred_element_type=F32).astype(BF16)


def finish_kernel(order, merged_ref, cols_ref, new_ref, out_ref):
    returned = jnp.dot(picks(cols_ref[0, :, 2:3], new_ref.shape[0]), new_ref[...], preferred_element_type=F32)
    out_ref[...] = (merged_ref[0] + returned).astype(BF16).reshape(out_ref.shape)


def shards(
    edge_state,
    atom_state,
    edge_src,
    edge_tgt,
    reverse,
    w_in,
    w_out,
    edge_gain,
    atom_gain,
    atom_up,
    atom_down,
):
    count_src = lax.axis_size("src")
    count_tgt = lax.axis_size("tgt")
    groups = count_src // count_tgt
    edge_rows, width = edge_state.shape
    atoms = atom_state.shape[0]
    rows_sub = edge_rows // (groups * count_src)
    rows = count_src * rows_sub
    slices = max(1, 256 // rows_sub)
    tile = slices * rows_sub
    tiles = rows // tile
    row = lax.axis_index("src")
    order = jnp.stack([lax.rem(s - row % groups + groups, groups) for s in range(groups)]).astype(jnp.int32)

    def by_group(index):
        return index.reshape(count_src, groups, rows_sub).transpose(1, 0, 2).reshape(groups, rows)

    spot = reverse // (groups * rows_sub) * rows_sub + reverse % rows_sub
    targets = by_group(edge_tgt)
    columns = jnp.stack([by_group(edge_src), by_group(spot), targets, targets], axis=-1)
    lines = targets.reshape(groups, 1, rows)
    framed = edge_state.reshape(count_src, groups, rows_sub, width)
    layers = w_in.shape[0]
    whole = pl.BlockSpec(memory_space=pltpu.VMEM)

    starts, received, streams = [], [], []
    for s in range(groups):
        start = pl.pallas_call(
            start_kernel,
            name=f"start{s}",
            grid_spec=pltpu.PrefetchScalarGridSpec(
                num_scalar_prefetch=1,
                grid=(tiles,),
                in_specs=[
                    pl.BlockSpec((slices, None, rows_sub, width), lambda t, order, s=s: (t, order[s], 0, 0)),
                    pl.BlockSpec((1, tile, 4), lambda t, order, s=s: (order[s], t, 0)),
                    pl.BlockSpec((atoms, width), lambda t, order: (0, 0)),
                ],
                out_specs=pl.BlockSpec((tile, width), lambda t, order: (t, 0)),
            ),
            out_shape=jax.ShapeDtypeStruct((rows, width), BF16),
        )(order, framed, columns, atom_state)
        pairs = []
        for i in range(count_src):
            for j in range(count_tgt):
                to = (j * groups + (s - i) % groups) * count_tgt + i // groups
                pairs.append((i * count_tgt + j, to))
        starts.append(start)
        received.append(lax.ppermute(start, ("src", "tgt"), pairs))
    wide = min(rows, 512)
    for s in range(groups):
        streams.append(
            pl.pallas_call(
                stream_kernel,
                name=f"stream{s}",
                grid=(rows // wide,),
                in_specs=[
                    pl.BlockSpec((wide, width), lambda t: (t, 0)),
                    pl.BlockSpec(w_in.shape, lambda t: (0, 0, 0)),
                    pl.BlockSpec(w_out.shape, lambda t: (0, 0, 0)),
                    pl.BlockSpec(edge_gain.shape, lambda t: (0, 0)),
                ],
                out_specs=pl.BlockSpec((wide, width), lambda t: (t, 0)),
                out_shape=jax.ShapeDtypeStruct((rows, width), F32),
                cost_estimate=pl.CostEstimate(
                    flops=4 * layers * rows * width * width,
                    bytes_accessed=6 * rows * width + 4 * layers * width * width,
                    transcendentals=layers * rows * width,
                ),
            )(starts[s], w_in, w_out, edge_gain)
        )
    merged, part = pl.pallas_call(
        functools.partial(merge_kernel, groups),
        name="merge",
        grid_spec=pltpu.PrefetchScalarGridSpec(
            num_scalar_prefetch=1,
            grid=(groups, tiles),
            in_specs=[
                pl.BlockSpec((tile, width), lambda g, t, order, s=s: (jnp.where(g == s, t, jnp.where(g < s, 0, tiles - 1)), 0))
                for s in range(groups)
            ]
            + [pl.BlockSpec((rows, width), lambda g, t, order: (0, 0)) for s in range(groups)]
            + [
                pl.BlockSpec((1, tile, 4), lambda g, t, order: (order[g], t, 0)),
                pl.BlockSpec((1, 1, tile), lambda g, t, order: (order[g], 0, t)),
            ],
            out_specs=[
                pl.BlockSpec((1, tile, width), lambda g, t, order: (g, t, 0)),
                pl.BlockSpec((1, atoms, width), lambda g, t, order: (order[g], 0, 0)),
            ],
            scratch_shapes=[pltpu.VMEM((atoms, width), F32)],
        ),
        out_shape=[
            jax.ShapeDtypeStruct((groups, rows, width), F32),
            jax.ShapeDtypeStruct((groups, atoms, width), BF16),
        ],
    )(order, *streams, *received, columns, lines)
    summed = lax.psum_scatter(part.reshape(groups * atoms, width), "src", scatter_dimension=0, tiled=True)
    updated = pl.pallas_call(
        atom_kernel,
        name="atoms",
        in_specs=[whole] * 4,
        out_specs=whole,
        out_shape=jax.ShapeDtypeStruct(summed.shape, BF16),
    )(summed, atom_gain.reshape(1, width), atom_up, atom_down)
    returned = lax.all_gather(updated, "src", axis=0, tiled=True)
    out = pl.pallas_call(
        finish_kernel,
        name="finish",
        grid_spec=pltpu.PrefetchScalarGridSpec(
            num_scalar_prefetch=1,
            grid=(groups, tiles),
            in_specs=[
                pl.BlockSpec((1, tile, width), lambda g, t, order: (g, t, 0)),
                pl.BlockSpec((1, tile, 4), lambda g, t, order: (order[g], t, 0)),
                pl.BlockSpec((atoms, width), lambda g, t, order: (order[g], 0)),
            ],
            out_specs=pl.BlockSpec((slices, None, rows_sub, width), lambda g, t, order: (t, order[g], 0, 0)),
        ),
        out_shape=jax.ShapeDtypeStruct(framed.shape, BF16),
    )(order, merged, columns, returned)
    return out.reshape(edge_rows, width)


def solution(mesh):
    in_specs = (
        P(("src", "tgt"), None),
        P("src", None),
        P(("src", "tgt")),
        P(("src", "tgt")),
        P(("src", "tgt")),
        P(),
        P(),
        P(),
        P(),
        P(),
        P(),
    )
    out_specs = P(("src", "tgt"), None)
    return jax.shard_map(shards, mesh=mesh, in_specs=in_specs, out_specs=out_specs, check_vma=False)
```

```python
import functools

import jax
import jax.numpy as jnp
from jax import lax
from jax.experimental import pallas as pl
from jax.experimental.pallas import tpu as pltpu
from jax.sharding import PartitionSpec as P

F32 = jnp.float32
BF16 = jnp.bfloat16


def rms_scaled(values, scales):
    return values * lax.rsqrt(jnp.mean(values * values, axis=-1, keepdims=True) + 1e-06) * scales


def picks(column, width):
    slots = lax.broadcasted_iota(jnp.int32, (column.shape[0], width), 1)
    return jnp.where(slots == column, 1.0, 0.0).astype(BF16)


def start_kernel(order, edge_ref, cols_ref, atom_ref, start_ref):
    rows, width = start_ref.shape
    sources = jnp.dot(picks(cols_ref[0, :, 0:1], atom_ref.shape[0]), atom_ref[...], preferred_element_type=F32)
    edges = edge_ref[...].reshape(rows, width).astype(F32)
    start_ref[...] = (edges + sources).astype(BF16)


def stream_kernel(start_ref, w_in_ref, w_out_ref, gain_ref, u_ref):
    stream = start_ref[...].astype(F32)
    for layer in range(w_in_ref.shape[0]):
        normed = rms_scaled(stream, gain_ref[layer : layer + 1]).astype(BF16)
        hidden = jax.nn.silu(jnp.dot(normed, w_in_ref[layer], preferred_element_type=F32)).astype(BF16)
        stream = stream + jnp.dot(hidden, w_out_ref[layer], preferred_element_type=F32)
    u_ref[...] = stream


def merge_kernel(groups, order, *refs):
    u_refs, recv_refs = refs[:groups], refs[groups : 2 * groups]
    cols_ref, tgt_ref, merged_ref, part_ref, total = refs[2 * groups :]
    turn, tile = pl.program_id(0), pl.program_id(1)

    @pl.when(tile == 0)
    def _():
        total[...] = jnp.zeros_like(total)

    for s in range(groups):

        @pl.when(turn == s)
        def _():
            partner = jnp.dot(
                picks(cols_ref[0, :, 1:2], recv_refs[s].shape[0]), recv_refs[s][...], preferred_element_type=F32
            )
            merged = u_refs[s][...] + partner
            merged_ref[0] = merged
            slots = lax.broadcasted_iota(jnp.int32, (total.shape[0], merged.shape[0]), 0)
            chosen = jnp.where(slots == tgt_ref[0], 1.0, 0.0).astype(BF16)
            total[...] += jnp.dot(chosen, merged.astype(BF16), preferred_element_type=F32)

    @pl.when(tile == pl.num_programs(1) - 1)
    def _():
        part_ref[0] = total[...].astype(part_ref.dtype)


def exchange_kernel(count, part_ref, gain_ref, up_ref, down_ref, new_ref, inbox, sent, landed, sent_new, landed_new):
    me = lax.axis_index("src")
    piece = part_ref.shape[0] // count

    def slot(owner):
        return pl.ds(pl.multiple_of(owner * piece, piece), piece)

    peers = [lax.rem(me + step, count) for step in range(1, count)]
    barrier = pltpu.get_barrier_semaphore()
    for peer in peers:
        pl.semaphore_signal(barrier, inc=1, device_id={"src": peer}, device_id_type=pl.DeviceIdType.MESH)
    pl.semaphore_wait(barrier, count - 1)
    shares = []
    for step, peer in enumerate(peers):
        share = pltpu.make_async_remote_copy(
            src_ref=part_ref.at[slot(peer)],
            dst_ref=inbox.at[step],
            send_sem=sent.at[step],
            recv_sem=landed.at[step],
            device_id={"src": peer},
            device_id_type=pl.DeviceIdType.MESH,
        )
        share.start()
        shares.append(share)
    total = part_ref[slot(me)].astype(F32)
    for step, share in enumerate(shares):
        share.wait_recv()
        total = total + inbox[step].astype(F32)
    normed = rms_scaled(total, gain_ref[...]).astype(BF16)
    hidden = jax.nn.silu(jnp.dot(normed, up_ref[...], preferred_element_type=F32)).astype(BF16)
    new_ref[slot(me)] = jnp.dot(hidden, down_ref[...], preferred_element_type=F32).astype(BF16)
    spreads = []
    for step, peer in enumerate(peers):
        spread = pltpu.make_async_remote_copy(
            src_ref=new_ref.at[slot(me)],
            dst_ref=new_ref.at[slot(me)],
            send_sem=sent_new.at[step],
            recv_sem=landed_new.at[step],
            device_id={"src": peer},
            device_id_type=pl.DeviceIdType.MESH,
        )
        spread.start()
        spreads.append(spread)
    for share in shares:
        share.wait_send()
    for spread in spreads:
        spread.wait()


def finish_kernel(order, merged_ref, cols_ref, new_ref, out_ref):
    returned = jnp.dot(picks(cols_ref[0, :, 2:3], new_ref.shape[0]), new_ref[...], preferred_element_type=F32)
    out_ref[...] = (merged_ref[0] + returned).astype(BF16).reshape(out_ref.shape)


def shards(
    edge_state,
    atom_state,
    edge_src,
    edge_tgt,
    reverse,
    w_in,
    w_out,
    edge_gain,
    atom_gain,
    atom_up,
    atom_down,
):
    count_src = lax.axis_size("src")
    count_tgt = lax.axis_size("tgt")
    groups = count_src // count_tgt
    edge_rows, width = edge_state.shape
    atoms = atom_state.shape[0]
    rows_sub = edge_rows // (groups * count_src)
    rows = count_src * rows_sub
    slices = max(1, 256 // rows_sub)
    tile = slices * rows_sub
    tiles = rows // tile
    row = lax.axis_index("src")
    order = jnp.stack([lax.rem(s - row % groups + groups, groups) for s in range(groups)]).astype(jnp.int32)

    def by_group(index):
        return index.reshape(count_src, groups, rows_sub).transpose(1, 0, 2).reshape(groups, rows)

    spot = reverse // (groups * rows_sub) * rows_sub + reverse % rows_sub
    targets = by_group(edge_tgt)
    columns = jnp.stack([by_group(edge_src), by_group(spot), targets, targets], axis=-1)
    lines = targets.reshape(groups, 1, rows)
    framed = edge_state.reshape(count_src, groups, rows_sub, width)
    layers = w_in.shape[0]
    whole = pl.BlockSpec(memory_space=pltpu.VMEM)

    starts, received, streams = [], [], []
    for s in range(groups):
        start = pl.pallas_call(
            start_kernel,
            name=f"start{s}",
            grid_spec=pltpu.PrefetchScalarGridSpec(
                num_scalar_prefetch=1,
                grid=(tiles,),
                in_specs=[
                    pl.BlockSpec((slices, None, rows_sub, width), lambda t, order, s=s: (t, order[s], 0, 0)),
                    pl.BlockSpec((1, tile, 4), lambda t, order, s=s: (order[s], t, 0)),
                    pl.BlockSpec((atoms, width), lambda t, order: (0, 0)),
                ],
                out_specs=pl.BlockSpec((tile, width), lambda t, order: (t, 0)),
            ),
            out_shape=jax.ShapeDtypeStruct((rows, width), BF16),
        )(order, framed, columns, atom_state)
        pairs = []
        for i in range(count_src):
            for j in range(count_tgt):
                to = (j * groups + (s - i) % groups) * count_tgt + i // groups
                pairs.append((i * count_tgt + j, to))
        starts.append(start)
        received.append(lax.ppermute(start, ("src", "tgt"), pairs))
    wide = min(rows, 512)
    for s in range(groups):
        streams.append(
            pl.pallas_call(
                stream_kernel,
                name=f"stream{s}",
                grid=(rows // wide,),
                in_specs=[
                    pl.BlockSpec((wide, width), lambda t: (t, 0)),
                    pl.BlockSpec(w_in.shape, lambda t: (0, 0, 0)),
                    pl.BlockSpec(w_out.shape, lambda t: (0, 0, 0)),
                    pl.BlockSpec(edge_gain.shape, lambda t: (0, 0)),
                ],
                out_specs=pl.BlockSpec((wide, width), lambda t: (t, 0)),
                out_shape=jax.ShapeDtypeStruct((rows, width), F32),
                cost_estimate=pl.CostEstimate(
                    flops=4 * layers * rows * width * width,
                    bytes_accessed=6 * rows * width + 4 * layers * width * width,
                    transcendentals=layers * rows * width,
                ),
            )(starts[s], w_in, w_out, edge_gain)
        )
    merged, part = pl.pallas_call(
        functools.partial(merge_kernel, groups),
        name="merge",
        grid_spec=pltpu.PrefetchScalarGridSpec(
            num_scalar_prefetch=1,
            grid=(groups, tiles),
            in_specs=[
                pl.BlockSpec((tile, width), lambda g, t, order, s=s: (jnp.where(g == s, t, jnp.where(g < s, 0, tiles - 1)), 0))
                for s in range(groups)
            ]
            + [pl.BlockSpec((rows, width), lambda g, t, order: (0, 0)) for s in range(groups)]
            + [
                pl.BlockSpec((1, tile, 4), lambda g, t, order: (order[g], t, 0)),
                pl.BlockSpec((1, 1, tile), lambda g, t, order: (order[g], 0, t)),
            ],
            out_specs=[
                pl.BlockSpec((1, tile, width), lambda g, t, order: (g, t, 0)),
                pl.BlockSpec((1, atoms, width), lambda g, t, order: (order[g], 0, 0)),
            ],
            scratch_shapes=[pltpu.VMEM((atoms, width), F32)],
        ),
        out_shape=[
            jax.ShapeDtypeStruct((groups, rows, width), F32),
            jax.ShapeDtypeStruct((groups, atoms, width), BF16),
        ],
    )(order, *streams, *received, columns, lines)
    piece = groups * atoms // count_src
    links = pltpu.SemaphoreType.DMA((count_src - 1,))
    returned = pl.pallas_call(
        functools.partial(exchange_kernel, count_src),
        name="exchange",
        in_specs=[whole] * 4,
        out_specs=whole,
        out_shape=jax.ShapeDtypeStruct((groups * atoms, width), BF16),
        scratch_shapes=[pltpu.VMEM((count_src - 1, piece, width), BF16), links, links, links, links],
        compiler_params=pltpu.CompilerParams(collective_id=0, has_side_effects=True),
    )(part.reshape(groups * atoms, width), atom_gain.reshape(1, width), atom_up, atom_down)
    out = pl.pallas_call(
        finish_kernel,
        name="finish",
        grid_spec=pltpu.PrefetchScalarGridSpec(
            num_scalar_prefetch=1,
            grid=(groups, tiles),
            in_specs=[
                pl.BlockSpec((1, tile, width), lambda g, t, order: (g, t, 0)),
                pl.BlockSpec((1, tile, 4), lambda g, t, order: (order[g], t, 0)),
                pl.BlockSpec((atoms, width), lambda g, t, order: (order[g], 0)),
            ],
            out_specs=pl.BlockSpec((slices, None, rows_sub, width), lambda g, t, order: (t, order[g], 0, 0)),
        ),
        out_shape=jax.ShapeDtypeStruct(framed.shape, BF16),
    )(order, merged, columns, returned)
    return out.reshape(edge_rows, width)


def solution(mesh):
    in_specs = (
        P(("src", "tgt"), None),
        P("src", None),
        P(("src", "tgt")),
        P(("src", "tgt")),
        P(("src", "tgt")),
        P(),
        P(),
        P(),
        P(),
        P(),
        P(),
    )
    out_specs = P(("src", "tgt"), None)
    return jax.shard_map(shards, mesh=mesh, in_specs=in_specs, out_specs=out_specs, check_vma=False)
```

```python
import functools

import jax
import jax.numpy as jnp
from jax import lax
from jax.experimental import pallas as pl
from jax.experimental.pallas import tpu as pltpu
from jax.sharding import PartitionSpec as P

F32 = jnp.float32
BF16 = jnp.bfloat16


def rms_scaled(values, scales):
    return values * lax.rsqrt(jnp.mean(values * values, axis=-1, keepdims=True) + 1e-06) * scales


def picks(column, width):
    slots = lax.broadcasted_iota(jnp.int32, (column.shape[0], width), 1)
    return jnp.where(slots == column, 1.0, 0.0).astype(BF16)


def start_kernel(order, edge_ref, cols_ref, atom_ref, start_ref):
    rows, width = start_ref.shape
    sources = jnp.dot(picks(cols_ref[0, :, 0:1], atom_ref.shape[0]), atom_ref[...], preferred_element_type=F32)
    edges = edge_ref[...].reshape(rows, width).astype(F32)
    start_ref[...] = (edges + sources).astype(BF16)


def stream_kernel(start_ref, w_in_ref, w_out_ref, gain_ref, u_ref):
    stream = start_ref[...].astype(F32)
    for layer in range(w_in_ref.shape[0]):
        normed = rms_scaled(stream, gain_ref[layer : layer + 1]).astype(BF16)
        hidden = jax.nn.silu(jnp.dot(normed, w_in_ref[layer], preferred_element_type=F32)).astype(BF16)
        stream = stream + jnp.dot(hidden, w_out_ref[layer], preferred_element_type=F32)
    u_ref[...] = stream


def merge_kernel(groups, order, *refs):
    u_refs, recv_refs = refs[:groups], refs[groups : 2 * groups]
    cols_ref, tgt_ref, merged_ref, part_ref, total = refs[2 * groups :]
    turn, tile = pl.program_id(0), pl.program_id(1)

    @pl.when(tile == 0)
    def _():
        total[...] = jnp.zeros_like(total)

    for s in range(groups):

        @pl.when(turn == s)
        def _():
            partner = jnp.dot(
                picks(cols_ref[0, :, 1:2], recv_refs[s].shape[0]), recv_refs[s][...], preferred_element_type=F32
            )
            merged = u_refs[s][...] + partner
            merged_ref[0] = merged
            slots = lax.broadcasted_iota(jnp.int32, (total.shape[0], merged.shape[0]), 0)
            chosen = jnp.where(slots == tgt_ref[0], 1.0, 0.0).astype(BF16)
            total[...] += jnp.dot(chosen, merged.astype(BF16), preferred_element_type=F32)

    @pl.when(tile == pl.num_programs(1) - 1)
    def _():
        part_ref[0] = total[...].astype(part_ref.dtype)


def exchange_kernel(
    count, part_ref, gain_ref, up_ref, down_ref, new_ref, near, far, paired, near_sems, far_sems, spread_sems, relay_sems
):
    me = lax.axis_index("src")
    piece = part_ref.shape[0] // count
    lines = count // 2
    place, side = me // 2, lax.rem(me, 2)
    partner = me + 1 - 2 * side

    def slot(owner):
        return pl.ds(pl.multiple_of(owner * piece, piece), piece)

    def send(source, target, sems, index, peer):
        copy = pltpu.make_async_remote_copy(
            src_ref=source,
            dst_ref=target,
            send_sem=sems.at[0, index],
            recv_sem=sems.at[1, index],
            device_id={"src": peer},
            device_id_type=pl.DeviceIdType.MESH,
        )
        copy.start()
        return copy

    ahead = [lax.rem(place + step, lines) for step in range(1, lines)] + [place]
    behind = [lax.rem(place - step + lines, lines) for step in range(1, lines)]
    barrier = pltpu.get_barrier_semaphore()
    for peer in [partner] + [spot * 2 + side for spot in ahead[:-1]]:
        pl.semaphore_signal(barrier, inc=1, device_id={"src": peer}, device_id_type=pl.DeviceIdType.MESH)
    pl.semaphore_wait(barrier, lines)

    shares = [
        send(part_ref.at[slot(spot * 2 + 1 - side)], near.at[step], near_sems, step, partner)
        for step, spot in enumerate(ahead)
    ]
    sums = []
    for step, spot in enumerate(ahead):
        shares[step].wait_recv()
        total = part_ref[slot(spot * 2 + side)].astype(F32) + near[step].astype(F32)
        if step < lines - 1:
            paired[step] = total.astype(BF16)
            sums.append(send(paired.at[step], far.at[step], far_sems, step, spot * 2 + side))
    for step in range(lines - 1):
        sums[step].wait_recv()
        total = total + far[step].astype(F32)
    normed = rms_scaled(total, gain_ref[...]).astype(BF16)
    hidden = jax.nn.silu(jnp.dot(normed, up_ref[...], preferred_element_type=F32)).astype(BF16)
    new_ref[slot(me)] = jnp.dot(hidden, down_ref[...], preferred_element_type=F32).astype(BF16)

    own = new_ref.at[slot(me)]
    spreads = [
        send(own, own, spread_sems, step, spot * 2 + side) for step, spot in enumerate(ahead[:-1])
    ]
    relays = [send(own, own, relay_sems, lines - 1, partner)]
    for step, spot in enumerate(behind):
        spreads[step].wait_recv()
        block = new_ref.at[slot(spot * 2 + side)]
        relays.append(send(block, block, relay_sems, step, partner))
    for copy in shares + sums + spreads:
        copy.wait_send()
    for copy in relays:
        copy.wait()


def finish_kernel(order, merged_ref, cols_ref, new_ref, out_ref):
    returned = jnp.dot(picks(cols_ref[0, :, 2:3], new_ref.shape[0]), new_ref[...], preferred_element_type=F32)
    out_ref[...] = (merged_ref[0] + returned).astype(BF16).reshape(out_ref.shape)


def shards(
    edge_state,
    atom_state,
    edge_src,
    edge_tgt,
    reverse,
    w_in,
    w_out,
    edge_gain,
    atom_gain,
    atom_up,
    atom_down,
):
    count_src = lax.axis_size("src")
    count_tgt = lax.axis_size("tgt")
    groups = count_src // count_tgt
    edge_rows, width = edge_state.shape
    atoms = atom_state.shape[0]
    rows_sub = edge_rows // (groups * count_src)
    rows = count_src * rows_sub
    slices = max(1, 256 // rows_sub)
    tile = slices * rows_sub
    tiles = rows // tile
    row = lax.axis_index("src")
    order = jnp.stack([lax.rem(s - row % groups + groups, groups) for s in range(groups)]).astype(jnp.int32)

    def by_group(index):
        return index.reshape(count_src, groups, rows_sub).transpose(1, 0, 2).reshape(groups, rows)

    spot = reverse // (groups * rows_sub) * rows_sub + reverse % rows_sub
    targets = by_group(edge_tgt)
    columns = jnp.stack([by_group(edge_src), by_group(spot), targets, targets], axis=-1)
    lines = targets.reshape(groups, 1, rows)
    framed = edge_state.reshape(count_src, groups, rows_sub, width)
    layers = w_in.shape[0]
    whole = pl.BlockSpec(memory_space=pltpu.VMEM)

    starts, received, streams = [], [], []
    for s in range(groups):
        start = pl.pallas_call(
            start_kernel,
            name=f"start{s}",
            grid_spec=pltpu.PrefetchScalarGridSpec(
                num_scalar_prefetch=1,
                grid=(tiles,),
                in_specs=[
                    pl.BlockSpec((slices, None, rows_sub, width), lambda t, order, s=s: (t, order[s], 0, 0)),
                    pl.BlockSpec((1, tile, 4), lambda t, order, s=s: (order[s], t, 0)),
                    pl.BlockSpec((atoms, width), lambda t, order: (0, 0)),
                ],
                out_specs=pl.BlockSpec((tile, width), lambda t, order: (t, 0)),
            ),
            out_shape=jax.ShapeDtypeStruct((rows, width), BF16),
        )(order, framed, columns, atom_state)
        pairs = []
        for i in range(count_src):
            for j in range(count_tgt):
                to = (j * groups + (s - i) % groups) * count_tgt + i // groups
                pairs.append((i * count_tgt + j, to))
        starts.append(start)
        received.append(lax.ppermute(start, ("src", "tgt"), pairs))
    wide = min(rows, 512)
    for s in range(groups):
        streams.append(
            pl.pallas_call(
                stream_kernel,
                name=f"stream{s}",
                grid=(rows // wide,),
                in_specs=[
                    pl.BlockSpec((wide, width), lambda t: (t, 0)),
                    pl.BlockSpec(w_in.shape, lambda t: (0, 0, 0)),
                    pl.BlockSpec(w_out.shape, lambda t: (0, 0, 0)),
                    pl.BlockSpec(edge_gain.shape, lambda t: (0, 0)),
                ],
                out_specs=pl.BlockSpec((wide, width), lambda t: (t, 0)),
                out_shape=jax.ShapeDtypeStruct((rows, width), F32),
                cost_estimate=pl.CostEstimate(
                    flops=4 * layers * rows * width * width,
                    bytes_accessed=6 * rows * width + 4 * layers * width * width,
                    transcendentals=layers * rows * width,
                ),
            )(starts[s], w_in, w_out, edge_gain)
        )
    merged, part = pl.pallas_call(
        functools.partial(merge_kernel, groups),
        name="merge",
        grid_spec=pltpu.PrefetchScalarGridSpec(
            num_scalar_prefetch=1,
            grid=(groups, tiles),
            in_specs=[
                pl.BlockSpec((tile, width), lambda g, t, order, s=s: (jnp.where(g == s, t, jnp.where(g < s, 0, tiles - 1)), 0))
                for s in range(groups)
            ]
            + [pl.BlockSpec((rows, width), lambda g, t, order: (0, 0)) for s in range(groups)]
            + [
                pl.BlockSpec((1, tile, 4), lambda g, t, order: (order[g], t, 0)),
                pl.BlockSpec((1, 1, tile), lambda g, t, order: (order[g], 0, t)),
            ],
            out_specs=[
                pl.BlockSpec((1, tile, width), lambda g, t, order: (g, t, 0)),
                pl.BlockSpec((1, atoms, width), lambda g, t, order: (order[g], 0, 0)),
            ],
            scratch_shapes=[pltpu.VMEM((atoms, width), F32)],
        ),
        out_shape=[
            jax.ShapeDtypeStruct((groups, rows, width), F32),
            jax.ShapeDtypeStruct((groups, atoms, width), BF16),
        ],
    )(order, *streams, *received, columns, lines)
    piece = groups * atoms // count_src
    lines_src = count_src // 2
    links = pltpu.SemaphoreType.DMA((2, lines_src))
    boxes = pltpu.VMEM((lines_src, piece, width), BF16)
    returned = pl.pallas_call(
        functools.partial(exchange_kernel, count_src),
        name="exchange",
        in_specs=[whole] * 4,
        out_specs=whole,
        out_shape=jax.ShapeDtypeStruct((groups * atoms, width), BF16),
        scratch_shapes=[boxes, boxes, boxes, links, links, links, links],
        compiler_params=pltpu.CompilerParams(collective_id=0, has_side_effects=True),
    )(part.reshape(groups * atoms, width), atom_gain.reshape(1, width), atom_up, atom_down)
    out = pl.pallas_call(
        finish_kernel,
        name="finish",
        grid_spec=pltpu.PrefetchScalarGridSpec(
            num_scalar_prefetch=1,
            grid=(groups, tiles),
            in_specs=[
                pl.BlockSpec((1, tile, width), lambda g, t, order: (g, t, 0)),
                pl.BlockSpec((1, tile, 4), lambda g, t, order: (order[g], t, 0)),
                pl.BlockSpec((atoms, width), lambda g, t, order: (order[g], 0)),
            ],
            out_specs=pl.BlockSpec((slices, None, rows_sub, width), lambda g, t, order: (t, order[g], 0, 0)),
        ),
        out_shape=jax.ShapeDtypeStruct(framed.shape, BF16),
    )(order, merged, columns, returned)
    return out.reshape(edge_rows, width)


def solution(mesh):
    in_specs = (
        P(("src", "tgt"), None),
        P("src", None),
        P(("src", "tgt")),
        P(("src", "tgt")),
        P(("src", "tgt")),
        P(),
        P(),
        P(),
        P(),
        P(),
        P(),
    )
    out_specs = P(("src", "tgt"), None)
    return jax.shard_map(shards, mesh=mesh, in_specs=in_specs, out_specs=out_specs, check_vma=False)
```
